256 devices in a mesh: section: 8 (over y, core), shard: 32 (over z, x).
Axes of the slice: x: 4, y: 4, z: 8, core: 2. Of those that a mesh axis runs over, the one named last changes fastest.
Arguments:
- activations: bfloat16 [8, 8, 32, 8192], P('section', None, None, 'shard'), may hold values from -6 to 6
- top_grad: bfloat16 [8, 32, 8192], P(None, None, 'shard'), may hold values from -6 to 6
- projection: bfloat16 [8, 8192, 8192], P('section', None, 'shard'), may hold values from -0.03125 to 0.03125
- basis_out: bfloat16 [8, 8192, 4096], P('section', None, 'shard'), may hold values from -0.0625 to 0.0625
- basis_in: bfloat16 [8, 8192, 4096], P('section', 'shard'), may hold values from -0.0625 to 0.0625
Outputs:
- eigenvalues: float32 [8, 4096, 4096], P('section', 'shard')
The draws below stay inside these ranges and needn't reach their ends.
All inputs are finite; a program needn't handle non-finite values.
Results may differ from the reference program's by a relative error of at most 0.007.
Values may be sent and summed in bfloat16 or wider, within the bound.
A program may use at most 64 MiB of HBM per device.

```python
import jax
import jax.numpy as jnp
from jax import lax

D = 8192
EIG_G = 4096
EIG_A = 4096
SEQ = 32
MICRO = 8
SECTIONS = 8


def levels(stream_key, dims, shards, smallest, high):
    loudness, own = 1.0, jax.random.fold_in(stream_key, 6)
    for position, shards_of in shards:
        steps = jnp.exp(jax.random.uniform(jax.random.fold_in(own, position), (shards_of,), jnp.float32, smallest / len(shards), high / len(shards)))
        loudness = loudness * jnp.repeat(steps, dims[position] // shards_of).reshape([-1 if axis == position else 1 for axis in range(len(dims))])
    return loudness


def noise(stream_key, shape, deviation, bound, split=(), dtype=jnp.bfloat16):
    drawn = deviation * jax.random.normal(stream_key, shape, jnp.float32)
    if split:
        drawn = drawn * levels(stream_key, shape, split, -0.22, 0.18)
    return jnp.clip(drawn, -bound, bound).astype(dtype)


def setup_inputs(seed: int = 0) -> dict:
    keys = jax.random.split(jax.random.key(seed), 6)
    activations = noise(keys[0], (SECTIONS, MICRO, SEQ, D), 1.0, 6.0, ((0, 8), (3, 32)))
    top_grad = noise(keys[1], (MICRO, SEQ, D), 1.0, 6.0, ((2, 32),))
    projection = noise(keys[2], (SECTIONS, D, D), (4 * D) ** -0.5, 0.03125, ((0, 8), (2, 32)))
    basis_out = noise(keys[3], (SECTIONS, D, EIG_G), D ** -0.5, 0.0625, ((0, 8), (2, 32)))
    basis_in = noise(keys[4], (SECTIONS, D, EIG_A), D ** -0.5, 0.0625, ((0, 8), (1, 32)))
    return {"activations": activations, "top_grad": top_grad, "projection": projection, "basis_out": basis_out, "basis_in": basis_in}


def reference(activations, top_grad, projection, basis_out, basis_in):
    grads = top_grad
    results = []
    for section_num in range(SECTIONS - 1, -1, -1):
        rot_in = jnp.einsum('msd,de->mse', activations[section_num].astype(jnp.float32), basis_in[section_num].astype(jnp.float32)).astype(jnp.bfloat16)
        rot_out = jnp.einsum('msd,dg->msg', grads.astype(jnp.float32), basis_out[section_num].astype(jnp.float32)).astype(jnp.bfloat16)
        rotated = jnp.einsum('msg,mse->mge', rot_out.astype(jnp.float32), rot_in.astype(jnp.float32)) / jnp.sqrt(jnp.float32(SEQ))
        results.append(lax.optimization_barrier(jnp.sum(rotated * rotated, axis=0)) / MICRO)
        through = jnp.einsum('msd,de->mse', grads.astype(jnp.float32), projection[section_num].astype(jnp.float32))
        grads = (grads.astype(jnp.float32) + through).astype(jnp.bfloat16)
    return jnp.stack(results[::-1])
```

```python
import functools

import jax
import jax.numpy as jnp
from jax import lax
from jax.experimental import pallas as pl
from jax.experimental.pallas import tpu as pltpu
from jax.sharding import Mesh
from jax.sharding import PartitionSpec as P

MESH = pl.DeviceIdType.MESH
SHARD = ("shard_0", "shard_1")
GROUPS = 8


def ring_order(size):
    near = [d for i in range(1, (size + 1) // 2) for d in (i, -i)]
    return [0] + near + ([size // 2] if size % 2 == 0 else [])


def chain_kernel(sections, nz, nx, groups, top, weight, basis, rot, gath, low, acc, accb,
                 z_recv, p_recv, m_recv, f_recv, t_send, z_send, x_send):
    k = lax.axis_index("section")
    z = lax.axis_index("shard_0")
    x = lax.axis_index("shard_1")
    offsets = ring_order(nz)
    width = weight.shape[1]
    right, left = lax.rem(x + 1, nx), lax.rem(x + nx - 1, nx)
    across = lax.rem(x + 2, nx)
    first = k == sections - 1
    inner = k < sections - 1
    passes = k > 0

    def at_z(offset):
        return lax.rem(z + offset + nz, nz)

    def copy(src, dst, send, recv, device):
        return pltpu.make_async_remote_copy(
            src_ref=src, dst_ref=dst, send_sem=send, recv_sem=recv,
            device_id=device, device_id_type=MESH,
        )

    barrier = pltpu.get_barrier_semaphore()

    def greet(device):
        pl.semaphore_signal(barrier, inc=1, device_id=device, device_id_type=MESH)

    greet((k, z, right))
    greet((k, z, left))

    @pl.when(passes)
    def _():
        for offset in offsets:
            greet((k - 1, at_z(offset), x))

    @pl.when(inner)
    def _():
        for offset in offsets:
            greet((k + 1, at_z(offset), x))

    @pl.when(first)
    def _():
        for offset in offsets[1:]:
            greet((k, at_z(offset), x))

    count = 2 + nz * passes.astype(jnp.int32) + nz * inner.astype(jnp.int32)
    pl.semaphore_wait(barrier, count + (nz - 1) * first.astype(jnp.int32))

    @pl.when(first)
    def _():
        def launch(g, carry):
            for i in reversed(range(1, nz)):
                copy(top.at[g], gath.at[g, x, z], t_send.at[g], z_recv.at[g, i],
                     (k, at_z(-offsets[i]), x)).start()
            gath[g, x, z] = top[g]
            return carry
        lax.fori_loop(0, groups, launch, 0)

    def multiply(g, column, table):
        total = None
        for zz in range(nz):
            start = pl.multiple_of((zz * nx + column) * width, width)
            part = jnp.dot(gath[g, column, zz], table[pl.ds(start, width), :],
                           preferred_element_type=jnp.float32)
            total = part if total is None else total + part
        return total

    def group_step(g, carry):
        for i, offset in enumerate(offsets):
            zz = at_z(offset)
            arrival = copy(low.at[g], gath.at[g, x, zz], z_send.at[g], z_recv.at[g, i], (k, z, x))
            if i == 0:
                pl.when(inner)(lambda: arrival.wait_recv())
            else:
                arrival.wait_recv()
            chunk = gath.at[g, x, zz]
            copy(chunk, chunk, x_send.at[g], p_recv.at[g, i], (k, z, right)).start()
            copy(chunk, chunk, x_send.at[g], m_recv.at[g, i], (k, z, left)).start()

        @pl.when(passes)
        def _():
            acc[...] = multiply(g, x, weight)

        for i, offset in enumerate(offsets):
            zz = at_z(offset)
            from_left, from_right = gath.at[g, left, zz], gath.at[g, right, zz]
            copy(from_left, from_left, x_send.at[g], p_recv.at[g, i], (k, z, right)).wait_recv()
            if i % 2 == 0:
                copy(from_left, from_left, x_send.at[g], f_recv.at[g], (k, z, right)).start()
            copy(from_right, from_right, x_send.at[g], m_recv.at[g, i], (k, z, left)).wait_recv()
            if i % 2 == 1:
                copy(from_right, from_right, x_send.at[g], f_recv.at[g], (k, z, left)).start()

        @pl.when(passes)
        def _():
            acc[...] += multiply(g, left, weight) + multiply(g, right, weight)

        far = gath.at[g, across]
        copy(far, far, x_send.at[g], f_recv.at[g], (k, z, right)).wait_recv()

        @pl.when(passes)
        def _():
            through = acc[...] + multiply(g, across, weight)
            low[g] = (gath[g, x, z].astype(jnp.float32) + through).astype(low.dtype)
            for i in reversed(range(nz)):
                copy(low.at[g], gath.at[g, x, z], z_send.at[g], z_recv.at[g, i],
                     (k - 1, at_z(-offsets[i]), x)).start()

        accb[...] = multiply(g, 0, basis) + multiply(g, 1, basis)
        rot[g] = (accb[...] + multiply(g, 2, basis) + multiply(g, 3, basis)).astype(rot.dtype)
        return carry

    lax.fori_loop(0, groups, group_step, 0)

    def drain(g, carry):
        sent = gath.at[g, pl.ds(0, nx - 1)]
        copy(sent, sent, x_send.at[g], f_recv.at[g], (k, z, right)).wait_send()

        @pl.when(passes)
        def _():
            column = gath.at[g, 0]
            copy(column, column, z_send.at[g], f_recv.at[g], (k, z, right)).wait_send()

        @pl.when(first)
        def _():
            column = gath.at[g, 0, pl.ds(0, nz - 1)]
            copy(column, column, t_send.at[g], f_recv.at[g], (k, z, right)).wait_send()
        return carry

    lax.fori_loop(0, groups, drain, 0)


def run_chain(sections, nz, nx, top, weight, basis):
    micro, seq, feat = top.shape
    groups = GROUPS
    rows = micro * seq // groups
    eig = basis.shape[1]
    dma = pltpu.SemaphoreType.DMA
    out = pl.pallas_call(
        functools.partial(chain_kernel, sections, nz, nx, groups),
        out_shape=jax.ShapeDtypeStruct((groups, rows, eig), jnp.bfloat16),
        in_specs=[pl.BlockSpec(memory_space=pltpu.VMEM)] * 3,
        out_specs=pl.BlockSpec(memory_space=pltpu.VMEM),
        scratch_shapes=[
            pltpu.VMEM((groups, nx, nz, rows, feat), jnp.bfloat16),
            pltpu.VMEM((groups, rows, feat), jnp.bfloat16),
            pltpu.VMEM((rows, feat), jnp.float32),
            pltpu.VMEM((rows, eig), jnp.float32),
            dma((groups, nz)), dma((groups, nz)), dma((groups, nz)), dma((groups,)),
            dma((groups,)), dma((groups,)), dma((groups,)),
        ],
        compiler_params=pltpu.CompilerParams(
            collective_id=0, has_side_effects=True, vmem_limit_bytes=40 << 20
        ),
        name="chain",
    )(top.reshape(groups, rows, feat), weight, basis)
    return out.reshape(micro, seq, eig)


def scatter_axes(value, axes, dim):
    for axis in axes:
        value = lax.psum_scatter(value, axis, scatter_dimension=dim, tiled=True)
    return value


def per_device(sections, nz, nx, activations, top_grad, projection, basis_out, basis_in):
    micro, seq_len = top_grad.shape[:2]
    scale = 1.0 / jnp.sqrt(jnp.float32(seq_len))
    partial_rot = jnp.einsum(
        "msd,de->mse", activations[0], basis_in[0], preferred_element_type=jnp.float32
    )
    share = scatter_axes(partial_rot, SHARD, 2).astype(jnp.bfloat16)
    rot_in = lax.all_gather(share, SHARD, axis=2, tiled=True)
    stored = run_chain(sections, nz, nx, top_grad, projection[0], basis_out[0])
    product = jnp.einsum("msg,mse->mge", stored, rot_in, preferred_element_type=jnp.float32) * scale
    summed = jnp.sum(product * product, axis=0)
    return (summed / micro)[None]


def solution(mesh):
    sections = mesh.shape["section"]
    nx = 4
    nz = mesh.shape["shard"] // nx
    finer = Mesh(mesh.devices.reshape(sections, nz, nx), ("section", "shard_0", "shard_1"))
    in_specs = (
        P("section", None, None, SHARD),
        P(None, None, SHARD),
        P("section", None, SHARD),
        P("section", None, SHARD),
        P("section", SHARD, None),
    )
    out_specs = P("section", SHARD, None)
    return jax.shard_map(
        functools.partial(per_device, sections, nz, nx), mesh=finer, in_specs=in_specs,
        out_specs=out_specs, check_vma=False,
    )
```

```python
import functools

import jax
import jax.numpy as jnp
from jax import lax
from jax.experimental import pallas as pl
from jax.experimental.pallas import tpu as pltpu
from jax.sharding import Mesh
from jax.sharding import PartitionSpec as P

MESH = pl.DeviceIdType.MESH
SHARD = ("shard_0", "shard_1")
GROUPS = 16
PAIR = 2
EARLY_SCATTER = 4
EARLY_GATHER = 4
VMEM_LIMIT = 56 << 20


def ring_order(size):
    near = [d for i in range(1, (size + 1) // 2) for d in (i, -i)]
    return [0] + near + ([size // 2] if size % 2 == 0 else [])


def fused_kernel(sections, nz, nx, groups, micro, act_hbm, top_hbm, weight_hbm, basis_hbm, in_hbm, out,
                 act, top, weight, basis, basis_in, gath, low, acc, rot, rot_t,
                 part, far_in, near_in, z_in, rot_in, load,
                 z_recv, p_recv, m_recv, f_recv, t_send, z_send, x_send,
                 rf_recv, rn_recv, rz_recv, rf_send, rn_send, rz_send,
                 az_recv, ap_recv, am_recv, af_recv, az_send, ax_send):
    k = lax.axis_index("section")
    z = lax.axis_index("shard_0")
    x = lax.axis_index("shard_1")
    loads = [
        pltpu.make_async_copy(src, dst, load.at[i])
        for i, (src, dst) in enumerate(
            ((top_hbm, top), (act_hbm, act), (in_hbm, basis_in), (weight_hbm, weight), (basis_hbm, basis))
        )
    ]
    for copy_in in loads:
        copy_in.start()
    offsets = ring_order(nz)
    spread = offsets[::-1]
    eig = basis.shape[1]
    width = weight.shape[1]
    right, left = lax.rem(x + 1, nx), lax.rem(x + nx - 1, nx)
    across = lax.rem(x + 2, nx)
    first = k == sections - 1
    inner = k < sections - 1
    passes = k > 0

    def at_z(offset):
        return lax.rem(z + offset + nz, nz)

    def copy(src, dst, send, recv, device):
        return pltpu.make_async_remote_copy(
            src_ref=src, dst_ref=dst, send_sem=send, recv_sem=recv,
            device_id=device, device_id_type=MESH,
        )

    barrier = pltpu.get_barrier_semaphore()

    def greet(device):
        pl.semaphore_signal(barrier, inc=1, device_id=device, device_id_type=MESH)

    for column in (right, left, across):
        greet((k, z, column))
    for offset in offsets[1:]:
        greet((k, at_z(offset), x))

    @pl.when(passes)
    def _():
        for offset in offsets:
            greet((k - 1, at_z(offset), x))

    @pl.when(inner)
    def _():
        for offset in offsets:
            greet((k + 1, at_z(offset), x))

    count = nx + nz - 2 + nz * passes.astype(jnp.int32) + nz * inner.astype(jnp.int32)
    pl.semaphore_wait(barrier, count)
    loads[0].wait()

    @pl.when(first)
    def _():
        def launch(g, carry):
            for i in reversed(range(1, nz)):
                copy(top.at[g], gath.at[g, x, z], t_send.at[g], z_recv.at[g, i],
                     (k, at_z(-offsets[i]), x)).start()
            gath[g, x, z] = top[g]
            return carry
        lax.fori_loop(0, groups, launch, 0)

    def multiply(g, column, table):
        total = None
        for zz in range(nz):
            start = pl.multiple_of((zz * nx + column) * width, width)
            part = jnp.dot(gath[g, column, zz], table[pl.ds(start, width), :],
                           preferred_element_type=jnp.float32)
            total = part if total is None else total + part
        return total

    def relay(g):
        for i, offset in enumerate(offsets):
            zz = at_z(offset)
            arrival = copy(low.at[g], gath.at[g, x, zz], z_send.at[g], z_recv.at[g, i], (k, z, x))
            if i == 0:
                pl.when(inner)(lambda: arrival.wait_recv())
            else:
                arrival.wait_recv()
            chunk = gath.at[g, x, zz]
            copy(chunk, chunk, x_send.at[g], f_recv.at[g], (k, z, across)).start()
            copy(chunk, chunk, x_send.at[g], p_recv.at[g], (k, z, right)).start()
            copy(chunk, chunk, x_send.at[g], m_recv.at[g], (k, z, left)).start()

    def finish(g):
        @pl.when(passes)
        def _():
            acc[...] = multiply(g, x, weight)

        for column, arrived in ((left, p_recv), (right, m_recv)):
            whole = gath.at[g, column]
            copy(whole, whole, x_send.at[g], arrived.at[g], (k, z, right)).wait_recv()

        @pl.when(passes)
        def _():
            acc[...] += multiply(g, left, weight) + multiply(g, right, weight)

        far = gath.at[g, across]
        copy(far, far, x_send.at[g], f_recv.at[g], (k, z, right)).wait_recv()

        @pl.when(passes)
        def _():
            through = acc[...] + multiply(g, across, weight)
            low[g] = (gath[g, x, z].astype(jnp.float32) + through).astype(low.dtype)
            for i in reversed(range(nz)):
                copy(low.at[g], gath.at[g, x, z], z_send.at[g], z_recv.at[g, i],
                     (k - 1, at_z(-offsets[i]), x)).start()

    def rotate(g, size):
        total = None
        for column in range(nx):
            for zz in range(nz):
                lhs = gath[pl.ds(g, size), column, zz]
                lhs = lhs.reshape(lhs.shape[0] * lhs.shape[1], width)
                part = jnp.dot(lhs, basis[(zz * nx + column) * width : (zz * nx + column + 1) * width, :],
                               preferred_element_type=jnp.float32)
                total = part if total is None else total + part
        rot[pl.ds(g, size)] = total.astype(rot.dtype).reshape(size, rot.shape[1], rot.shape[2])

    def group_step(g, carry):
        pl.when(g + 1 < groups)(lambda: relay(g + 1))
        finish(g)
        pl.when(lax.rem(g, PAIR) == PAIR - 1)(lambda: rotate(g - (PAIR - 1), PAIR))
        return carry

    def chain():
        relay(0)
        loads[3].wait()
        loads[4].wait()
        lax.fori_loop(0, groups, group_step, 0)

    def product(owner, zz):
        start = pl.multiple_of((owner * nz + zz) * eig, eig)
        piece = jnp.dot(act[...], basis_in[:, pl.ds(start, eig)], preferred_element_type=jnp.float32)
        part[owner, zz] = piece.astype(part.dtype)

    def reduce_scatter():
        loads[1].wait()
        loads[2].wait()
        for i, offset in enumerate(spread):
            zz = at_z(offset)
            product(across, zz)
            copy(part.at[across, zz], far_in.at[i], rf_send, rf_recv.at[i],
                 (k, z, left if i % 2 == 0 else right)).start()
        for i, offset in enumerate(spread):
            zz = at_z(offset)
            product(left, zz)
            product(right, zz)
            if i % 2 == 0:
                copy(part.at[right, zz], near_in.at[0, i], rn_send, rn_recv.at[0, i], (k, z, right)).start()
            else:
                copy(part.at[left, zz], near_in.at[1, i], rn_send, rn_recv.at[1, i], (k, z, left)).start()
        for i, offset in enumerate(spread):
            zz = at_z(offset)
            product(x, zz)
            copy(far_in.at[i], far_in.at[i], rf_send, rf_recv.at[i], (k, z, left)).wait_recv()
            if i % 2 == 0:
                part[left, zz] = add(part[left, zz], far_in[i])
                copy(part.at[left, zz], near_in.at[1, i], rn_send, rn_recv.at[1, i], (k, z, left)).start()
            else:
                part[right, zz] = add(part[right, zz], far_in[i])
                copy(part.at[right, zz], near_in.at[0, i], rn_send, rn_recv.at[0, i], (k, z, right)).start()
        for i, offset in enumerate(spread):
            zz = at_z(offset)
            for side in range(2):
                arrived = near_in.at[side, i]
                copy(arrived, arrived, rn_send, rn_recv.at[side, i], (k, z, left)).wait_recv()
            part[x, zz] = add(part[x, zz], near_in[0, i], near_in[1, i])
            if offset != 0:
                copy(part.at[x, zz], z_in.at[i], rz_send, rz_recv.at[i], (k, zz, x)).start()
        total = part[x, z].astype(jnp.float32)
        for i, offset in enumerate(spread):
            if offset != 0:
                copy(z_in.at[i], z_in.at[i], rz_send, rz_recv.at[i], (k, z, left)).wait_recv()
                total = total + z_in[i].astype(jnp.float32)
        rot_in[x, z] = total.astype(rot_in.dtype)

    def add(*terms):
        total = terms[0].astype(jnp.float32)
        for term in terms[1:]:
            total = total + term.astype(jnp.float32)
        return total.astype(part.dtype)

    def all_gather():
        mine = rot_in.at[x, z]
        for i in reversed(range(1, nz)):
            copy(mine, mine, az_send, az_recv.at[i], (k, at_z(-offsets[i]), x)).start()
        for i, offset in enumerate(offsets):
            piece = rot_in.at[x, at_z(offset)]
            if i > 0:
                copy(piece, piece, az_send, az_recv.at[i], (k, z, right)).wait_recv()
            copy(piece, piece, ax_send, ap_recv.at[i], (k, z, right)).start()
            copy(piece, piece, ax_send, am_recv.at[i], (k, z, left)).start()
        for i, offset in enumerate(offsets):
            zz = at_z(offset)
            from_left, from_right = rot_in.at[left, zz], rot_in.at[right, zz]
            copy(from_left, from_left, ax_send, ap_recv.at[i], (k, z, right)).wait_recv()
            if i % 2 == 0:
                copy(from_left, from_left, ax_send, af_recv, (k, z, right)).start()
            copy(from_right, from_right, ax_send, am_recv.at[i], (k, z, left)).wait_recv()
            if i % 2 == 1:
                copy(from_right, from_right, ax_send, af_recv, (k, z, left)).start()
        whole = rot_in.at[across]
        copy(whole, whole, ax_send, af_recv, (k, z, left)).wait_recv()

    scatter_stage = jnp.where(k < EARLY_SCATTER, 0, 2)
    gather_stage = jnp.where(k < EARLY_GATHER, 0, 2)

    def stage(index, carry):
        pl.when(index == scatter_stage)(reduce_scatter)
        pl.when(index == gather_stage)(all_gather)
        pl.when(index == 1)(chain)
        return carry

    lax.fori_loop(0, 3, stage, 0)

    seq = groups * low.shape[1] // micro
    per = groups // micro
    for m in range(micro):
        tokens = rot[m * per : (m + 1) * per].reshape(seq, eig)
        rot_t[m] = (tokens.astype(jnp.float32) * (1.0 / 16.0)).T.astype(rot_t.dtype)

    def square(step, carry):
        column, half = step // (nz // 2), lax.rem(step, nz // 2)
        total = None
        for m in range(micro):
            rows = pl.ds(m * seq, seq)
            rhs = jnp.concatenate(
                [rot_in[column, 2 * half, rows], rot_in[column, 2 * half + 1, rows]], axis=1
            )
            value = jnp.dot(rot_t[m], rhs, preferred_element_type=jnp.float32)
            total = value * value if total is None else total + value * value
        out[:, pl.ds(pl.multiple_of(step * 2 * eig, 2 * eig), 2 * eig)] = total
        return carry

    lax.fori_loop(0, nx * nz // 2, square, 0)

    for pieces, sem in (
        (part.at[0], rf_send), (part.at[pl.ds(0, 2)], rn_send), (part.at[0, pl.ds(0, nz - 1)], rz_send),
        (part.at[0, pl.ds(0, nz - 1)], az_send), (part.at[pl.ds(0, 3)], ax_send),
    ):
        copy(pieces, pieces, sem, af_recv, (k, z, right)).wait_send()

    def drain(g, carry):
        sent = gath.at[g, pl.ds(0, nx - 1)]
        copy(sent, sent, x_send.at[g], f_recv.at[g], (k, z, right)).wait_send()

        @pl.when(passes)
        def _():
            column = gath.at[g, 0]
            copy(column, column, z_send.at[g], f_recv.at[g], (k, z, right)).wait_send()

        @pl.when(first)
        def _():
            column = gath.at[g, 0, pl.ds(0, nz - 1)]
            copy(column, column, t_send.at[g], f_recv.at[g], (k, z, right)).wait_send()
        return carry

    lax.fori_loop(0, groups, drain, 0)


def run_fused(sections, nz, nx, act, top, weight, basis, basis_in):
    micro, seq, feat = top.shape
    groups = GROUPS
    tokens = micro * seq
    rows = tokens // groups
    eig = basis.shape[1]
    half = jnp.bfloat16
    dma = pltpu.SemaphoreType.DMA
    return pl.pallas_call(
        functools.partial(fused_kernel, sections, nz, nx, groups, micro),
        out_shape=jax.ShapeDtypeStruct((eig, nx * nz * eig), jnp.float32),
        in_specs=[pl.BlockSpec(memory_space=pl.ANY)] * 5,
        out_specs=pl.BlockSpec(memory_space=pltpu.VMEM),
        scratch_shapes=[
            pltpu.VMEM((tokens, feat), half),
            pltpu.VMEM((groups, rows, feat), half),
            pltpu.VMEM(weight.shape, half),
            pltpu.VMEM(basis.shape, half),
            pltpu.VMEM(basis_in.shape, half),
            pltpu.VMEM((groups, nx, nz, rows, feat), half),
            pltpu.VMEM((groups, rows, feat), half),
            pltpu.VMEM((rows, feat), jnp.float32),
            pltpu.VMEM((groups, rows, eig), half),
            pltpu.VMEM((micro, eig, seq), half),
            pltpu.VMEM((nx, nz, tokens, eig), half),
            pltpu.VMEM((nz, tokens, eig), half),
            pltpu.VMEM((2, nz, tokens, eig), half),
            pltpu.VMEM((nz, tokens, eig), half),
            pltpu.VMEM((nx, nz, tokens, eig), half),
            dma((5,)),
            dma((groups, nz)), dma((groups,)), dma((groups,)), dma((groups,)),
            dma((groups,)), dma((groups,)), dma((groups,)),
            dma((nz,)), dma((2, nz)), dma((nz,)), dma, dma, dma,
            dma((nz,)), dma((nz,)), dma((nz,)), dma, dma, dma,
        ],
        compiler_params=pltpu.CompilerParams(
            collective_id=0, has_side_effects=True, vmem_limit_bytes=VMEM_LIMIT
        ),
        name="fused",
    )(act.reshape(tokens, feat), top.reshape(groups, rows, feat), weight, basis, basis_in)


def per_device(sections, nz, nx, activations, top_grad, projection, basis_out, basis_in):
    return run_fused(
        sections, nz, nx, activations[0], top_grad, projection[0], basis_out[0], basis_in[0]
    )[None]


def solution(mesh):
    sections = mesh.shape["section"]
    nx = 4
    nz = mesh.shape["shard"] // nx
    finer = Mesh(mesh.devices.reshape(sections, nz, nx), ("section", "shard_0", "shard_1"))
    in_specs = (
        P("section", None, None, SHARD),
        P(None, None, SHARD),
        P("section", None, SHARD),
        P("section", None, SHARD),
        P("section", SHARD, None),
    )
    out_specs = P("section", SHARD, None)
    return jax.shard_map(
        functools.partial(per_device, sections, nz, nx), mesh=finer, in_specs=in_specs,
        out_specs=out_specs, check_vma=False,
    )
```

```python
import functools

import jax
import jax.numpy as jnp
from jax import lax
from jax.experimental import pallas as pl
from jax.experimental.pallas import tpu as pltpu
from jax.sharding import Mesh
from jax.sharding import PartitionSpec as P

MESH = pl.DeviceIdType.MESH
SHARD = ("shard_0", "shard_1")
GROUPS = 16
EARLY_SCATTER = 6
EARLY_GATHER = 2
AHEAD = 2
VMEM_LIMIT = 26 << 20


def ring_order(size):
    near = [d for i in range(1, (size + 1) // 2) for d in (i, -i)]
    return [0] + near + ([size // 2] if size % 2 == 0 else [])


def fused_kernel(sections, nz, nx, groups, micro, act_hbm, top_hbm, weight_hbm, basis_hbm, in_hbm, out,
                 act, top, weight, basis, basis_in, gath, low, acc, rot, rot_t,
                 part, far_in, near_in, z_in, rot_in, load,
                 z_recv, p_recv, m_recv, f_recv, t_send, z_send, x_send,
                 rf_recv, rn_recv, rz_recv, rf_send, rn_send, rz_send,
                 az_recv, ap_recv, am_recv, af_recv, az_send, ax_send):
    k = lax.axis_index("section")
    z = lax.axis_index("shard_0")
    x = lax.axis_index("shard_1")
    loads = [
        pltpu.make_async_copy(src, dst, load.at[i])
        for i, (src, dst) in enumerate(
            ((top_hbm, top), (act_hbm, act), (in_hbm, basis_in), (weight_hbm, weight), (basis_hbm, basis))
        )
    ]
    for copy_in in loads:
        copy_in.start()
    offsets = ring_order(nz)
    spread = offsets[::-1]
    eig = basis.shape[1]
    width = weight.shape[1]
    per = groups // micro
    seq = per * low.shape[1]
    scatter_stage = jnp.where(k < EARLY_SCATTER, 0, 2)
    gather_stage = jnp.where(k < EARLY_GATHER, 0, 2)
    right, left = lax.rem(x + 1, nx), lax.rem(x + nx - 1, nx)
    across = lax.rem(x + 2, nx)
    first = k == sections - 1
    inner = k < sections - 1
    passes = k > 0

    def at_z(offset):
        return lax.rem(z + offset + nz, nz)

    def copy(src, dst, send, recv, device):
        return pltpu.make_async_remote_copy(
            src_ref=src, dst_ref=dst, send_sem=send, recv_sem=recv,
            device_id=device, device_id_type=MESH,
        )

    barrier = pltpu.get_barrier_semaphore()

    def greet(device):
        pl.semaphore_signal(barrier, inc=1, device_id=device, device_id_type=MESH)

    for column in (right, left, across):
        greet((k, z, column))
    for offset in offsets[1:]:
        greet((k, at_z(offset), x))

    @pl.when(passes)
    def _():
        for offset in offsets:
            greet((k - 1, at_z(offset), x))

    @pl.when(inner)
    def _():
        for offset in offsets:
            greet((k + 1, at_z(offset), x))

    count = nx + nz - 2 + nz * passes.astype(jnp.int32) + nz * inner.astype(jnp.int32)
    pl.semaphore_wait(barrier, count)
    loads[0].wait()

    @pl.when(first)
    def _():
        def launch(g, carry):
            for i in reversed(range(1, nz)):
                copy(top.at[g], gath.at[g, x, z], t_send.at[g], z_recv.at[g, i],
                     (k, at_z(-offsets[i]), x)).start()
            gath[g, x, z] = top[g]
            return carry
        lax.fori_loop(0, groups, launch, 0)

    def multiply(g, column, table):
        total = None
        for zz in range(nz):
            start = pl.multiple_of((zz * nx + column) * width, width)
            part = jnp.dot(gath[g, column, zz], table[pl.ds(start, width), :],
                           preferred_element_type=jnp.float32)
            total = part if total is None else total + part
        return total

    def relay(g):
        for i, offset in enumerate(offsets):
            zz = at_z(offset)
            arrival = copy(low.at[g], gath.at[g, x, zz], z_send.at[g], z_recv.at[g, i], (k, z, x))
            if i == 0:
                pl.when(inner)(lambda: arrival.wait_recv())
            else:
                arrival.wait_recv()
            chunk = gath.at[g, x, zz]
            copy(chunk, chunk, x_send.at[g], f_recv.at[g], (k, z, across)).start()
            copy(chunk, chunk, x_send.at[g], p_recv.at[g], (k, z, right)).start()
            copy(chunk, chunk, x_send.at[g], m_recv.at[g], (k, z, left)).start()

    def finish(g):
        @pl.when(passes)
        def _():
            acc[...] = multiply(g, x, weight)

        for column, arrived in ((left, p_recv), (right, m_recv)):
            whole = gath.at[g, column]
            copy(whole, whole, x_send.at[g], arrived.at[g], (k, z, right)).wait_recv()

        @pl.when(passes)
        def _():
            acc[...] += multiply(g, left, weight) + multiply(g, right, weight)

        far = gath.at[g, across]
        copy(far, far, x_send.at[g], f_recv.at[g], (k, z, right)).wait_recv()

        @pl.when(passes)
        def _():
            through = acc[...] + multiply(g, across, weight)
            low[g] = (gath[g, x, z].astype(jnp.float32) + through).astype(low.dtype)
            for i in reversed(range(nz)):
                copy(low.at[g], gath.at[g, x, z], z_send.at[g], z_recv.at[g, i],
                     (k - 1, at_z(-offsets[i]), x)).start()

    def rotate(g, size):
        total = None
        for column in range(nx):
            for zz in range(nz):
                lhs = gath[pl.ds(g, size), column, zz]
                lhs = lhs.reshape(lhs.shape[0] * lhs.shape[1], width)
                part = jnp.dot(lhs, basis[(zz * nx + column) * width : (zz * nx + column + 1) * width, :],
                               preferred_element_type=jnp.float32)
                total = part if total is None else total + part
        rot[pl.ds(g, size)] = total.astype(rot.dtype).reshape(size, rot.shape[1], rot.shape[2])

    def rotated(m, column, half):
        rows = pl.ds(pl.multiple_of(m * seq, seq), seq)
        rhs = jnp.concatenate(
            [rot_in[column, 2 * half, rows], rot_in[column, 2 * half + 1, rows]], axis=1
        )
        return jnp.dot(rot_t[m], rhs, preferred_element_type=jnp.float32)

    def square_one(m):
        for step in range(nx * nz // 2):
            value = rotated(m, step // (nz // 2), step % (nz // 2))
            columns = slice(step * 2 * eig, (step + 1) * 2 * eig)
            before = jnp.where(m > 0, out[:, columns], 0.0)
            out[:, columns] = before + value * value

    def group_step(g, carry):
        pl.when(g + AHEAD < groups)(lambda: relay(g + AHEAD))
        finish(g)

        @pl.when(lax.rem(g, per) == per - 1)
        def _():
            m = g // per
            rotate(m * per, per)
            tokens = rot[pl.ds(m * per, per)].reshape(seq, eig)
            rot_t[m] = (tokens.astype(jnp.float32) * (1.0 / 16.0)).T.astype(rot_t.dtype)
            pl.when(gather_stage == 0)(lambda: square_one(m))
        return carry

    def chain():
        for early in range(AHEAD):
            relay(early)
        loads[3].wait()
        loads[4].wait()
        lax.fori_loop(0, groups, group_step, 0)

    def product(owner, zz):
        start = pl.multiple_of((owner * nz + zz) * eig, eig)
        piece = jnp.dot(act[...], basis_in[:, pl.ds(start, eig)], preferred_element_type=jnp.float32)
        part[owner, zz] = piece.astype(part.dtype)

    def reduce_scatter():
        loads[1].wait()
        loads[2].wait()
        for i, offset in enumerate(spread):
            zz = at_z(offset)
            product(across, zz)
            copy(part.at[across, zz], far_in.at[i], rf_send, rf_recv.at[i],
                 (k, z, left if i % 2 == 0 else right)).start()
        for i, offset in enumerate(spread):
            zz = at_z(offset)
            product(left, zz)
            product(right, zz)
            if i % 2 == 0:
                copy(part.at[right, zz], near_in.at[0, i], rn_send, rn_recv.at[0, i], (k, z, right)).start()
            else:
                copy(part.at[left, zz], near_in.at[1, i], rn_send, rn_recv.at[1, i], (k, z, left)).start()
        for i, offset in enumerate(spread):
            zz = at_z(offset)
            product(x, zz)
            copy(far_in.at[i], far_in.at[i], rf_send, rf_recv.at[i], (k, z, left)).wait_recv()
            if i % 2 == 0:
                part[left, zz] = add(part[left, zz], far_in[i])
                copy(part.at[left, zz], near_in.at[1, i], rn_send, rn_recv.at[1, i], (k, z, left)).start()
            else:
                part[right, zz] = add(part[right, zz], far_in[i])
                copy(part.at[right, zz], near_in.at[0, i], rn_send, rn_recv.at[0, i], (k, z, right)).start()
        for i, offset in enumerate(spread):
            zz = at_z(offset)
            for side in range(2):
                arrived = near_in.at[side, i]
                copy(arrived, arrived, rn_send, rn_recv.at[side, i], (k, z, left)).wait_recv()
            part[x, zz] = add(part[x, zz], near_in[0, i], near_in[1, i])
            if offset != 0:
                copy(part.at[x, zz], z_in.at[i], rz_send, rz_recv.at[i], (k, zz, x)).start()
        total = part[x, z].astype(jnp.float32)
        for i, offset in enumerate(spread):
            if offset != 0:
                copy(z_in.at[i], z_in.at[i], rz_send, rz_recv.at[i], (k, z, left)).wait_recv()
                total = total + z_in[i].astype(jnp.float32)
        rot_in[x, z] = total.astype(rot_in.dtype)

    def add(*terms):
        total = terms[0].astype(jnp.float32)
        for term in terms[1:]:
            total = total + term.astype(jnp.float32)
        return total.astype(part.dtype)

    def all_gather():
        mine = rot_in.at[x, z]
        for i in reversed(range(1, nz)):
            copy(mine, mine, az_send, az_recv.at[i], (k, at_z(-offsets[i]), x)).start()
        for i, offset in enumerate(offsets):
            piece = rot_in.at[x, at_z(offset)]
            if i > 0:
                copy(piece, piece, az_send, az_recv.at[i], (k, z, right)).wait_recv()
            copy(piece, piece, ax_send, ap_recv.at[i], (k, z, right)).start()
            copy(piece, piece, ax_send, am_recv.at[i], (k, z, left)).start()
        for i, offset in enumerate(offsets):
            zz = at_z(offset)
            from_left, from_right = rot_in.at[left, zz], rot_in.at[right, zz]
            copy(from_left, from_left, ax_send, ap_recv.at[i], (k, z, right)).wait_recv()
            if i % 2 == 0:
                copy(from_left, from_left, ax_send, af_recv, (k, z, right)).start()
            copy(from_right, from_right, ax_send, am_recv.at[i], (k, z, left)).wait_recv()
            if i % 2 == 1:
                copy(from_right, from_right, ax_send, af_recv, (k, z, left)).start()
        whole = rot_in.at[across]
        copy(whole, whole, ax_send, af_recv, (k, z, left)).wait_recv()

    def stage(index, carry):
        pl.when(index == scatter_stage)(reduce_scatter)
        pl.when(index == gather_stage)(all_gather)
        pl.when(index == 1)(chain)
        return carry

    lax.fori_loop(0, 3, stage, 0)

    @pl.when(gather_stage > 0)
    def _():
        def square(step, carry):
            total = None
            for m in range(micro):
                value = rotated(m, step // (nz // 2), lax.rem(step, nz // 2))
                total = value * value if total is None else total + value * value
            out[:, pl.ds(pl.multiple_of(step * 2 * eig, 2 * eig), 2 * eig)] = total
            return carry

        lax.fori_loop(0, nx * nz // 2, square, 0)

    for pieces, sem in (
        (part.at[0], rf_send), (part.at[pl.ds(0, 2)], rn_send), (part.at[0, pl.ds(0, nz - 1)], rz_send),
        (part.at[0, pl.ds(0, nz - 1)], az_send), (part.at[pl.ds(0, 3)], ax_send),
    ):
        copy(pieces, pieces, sem, af_recv, (k, z, right)).wait_send()

    def drain(g, carry):
        sent = gath.at[g, pl.ds(0, nx - 1)]
        copy(sent, sent, x_send.at[g], f_recv.at[g], (k, z, right)).wait_send()

        @pl.when(passes)
        def _():
            column = gath.at[g, 0]
            copy(column, column, z_send.at[g], f_recv.at[g], (k, z, right)).wait_send()

        @pl.when(first)
        def _():
            column = gath.at[g, 0, pl.ds(0, nz - 1)]
            copy(column, column, t_send.at[g], f_recv.at[g], (k, z, right)).wait_send()
        return carry

    lax.fori_loop(0, groups, drain, 0)


def run_fused(sections, nz, nx, act, top, weight, basis, basis_in):
    micro, seq, feat = top.shape
    groups = GROUPS
    tokens = micro * seq
    rows = tokens // groups
    eig = basis.shape[1]
    half = jnp.bfloat16
    dma = pltpu.SemaphoreType.DMA
    return pl.pallas_call(
        functools.partial(fused_kernel, sections, nz, nx, groups, micro),
        out_shape=jax.ShapeDtypeStruct((eig, nx * nz * eig), jnp.float32),
        in_specs=[pl.BlockSpec(memory_space=pltpu.HBM)] * 5,
        out_specs=pl.BlockSpec(memory_space=pltpu.VMEM),
        scratch_shapes=[
            pltpu.VMEM((tokens, feat), half),
            pltpu.VMEM((groups, rows, feat), half),
            pltpu.VMEM(weight.shape, half),
            pltpu.VMEM(basis.shape, half),
            pltpu.VMEM(basis_in.shape, half),
            pltpu.VMEM((groups, nx, nz, rows, feat), half),
            pltpu.VMEM((groups, rows, feat), half),
            pltpu.VMEM((rows, feat), jnp.float32),
            pltpu.VMEM((groups, rows, eig), half),
            pltpu.VMEM((micro, eig, seq), half),
            pltpu.VMEM((nx, nz, tokens, eig), half),
            pltpu.VMEM((nz, tokens, eig), half),
            pltpu.VMEM((2, nz, tokens, eig), half),
            pltpu.VMEM((nz, tokens, eig), half),
            pltpu.VMEM((nx, nz, tokens, eig), half),
            dma((5,)),
            dma((groups, nz)), dma((groups,)), dma((groups,)), dma((groups,)),
            dma((groups,)), dma((groups,)), dma((groups,)),
            dma((nz,)), dma((2, nz)), dma((nz,)), dma, dma, dma,
            dma((nz,)), dma((nz,)), dma((nz,)), dma, dma, dma,
        ],
        compiler_params=pltpu.CompilerParams(
            collective_id=0, has_side_effects=True, vmem_limit_bytes=VMEM_LIMIT
        ),
        name="fused",
    )(*(pltpu.with_memory_space_constraint(a, pltpu.HBM) for a in (
        act.reshape(tokens, feat), top.reshape(groups, rows, feat), weight, basis, basis_in)))


def per_device(sections, nz, nx, activations, top_grad, projection, basis_out, basis_in):
    return run_fused(
        sections, nz, nx, activations[0], top_grad, projection[0], basis_out[0], basis_in[0]
    )[None]


def solution(mesh):
    sections = mesh.shape["section"]
    nx = 4
    nz = mesh.shape["shard"] // nx
    finer = Mesh(mesh.devices.reshape(sections, nz, nx), ("section", "shard_0", "shard_1"))
    in_specs = (
        P("section", None, None, SHARD),
        P(None, None, SHARD),
        P("section", None, SHARD),
        P("section", None, SHARD),
        P("section", SHARD, None),
    )
    out_specs = P("section", SHARD, None)
    return jax.shard_map(
        functools.partial(per_device, sections, nz, nx), mesh=finer, in_specs=in_specs,
        out_specs=out_specs, check_vma=False,
    )
```

```python
import functools

import jax
import jax.numpy as jnp
from jax import lax
from jax.experimental import pallas as pl
from jax.experimental.pallas import tpu as pltpu
from jax.sharding import Mesh
from jax.sharding import PartitionSpec as P

MESH = pl.DeviceIdType.MESH
SHARD = ("shard_0", "shard_1")
GROUPS = 16
EARLY_SCATTER = 6
EARLY_GATHER = 2
AHEAD = 2
LAUNCH = 4
VMEM_LIMIT = 26 << 20
PAIRED = {0: 1, 1: 1, 2: -1}


def ring_order(size):
    near = [d for i in range(1, (size + 1) // 2) for d in (i, -i)]
    return [0] + near + ([size // 2] if size % 2 == 0 else [])


def fused_kernel(sections, nz, nx, groups, micro, act_hbm, top_hbm, weight_hbm, basis_hbm, in_hbm, out,
                 act, top, weight, basis, basis_in, gath, low, acc, rot, rot_t,
                 part, far_in, near_in, z_in, rot_in, load,
                 z_recv, b_recv, p_recv, m_recv, f_recv, t_send, z_send, x_send,
                 rf_recv, rn_recv, rz_recv, rf_send, rn_send, rz_send,
                 az_recv, ap_recv, am_recv, af_recv, az_send, ax_send):
    k = lax.axis_index("section")
    z = lax.axis_index("shard_0")
    x = lax.axis_index("shard_1")
    loads = [
        pltpu.make_async_copy(src, dst, load.at[i])
        for i, (src, dst) in enumerate(
            ((top_hbm, top), (act_hbm, act), (in_hbm, basis_in), (weight_hbm, weight), (basis_hbm, basis))
        )
    ]
    for copy_in in loads:
        copy_in.start()
    offsets = ring_order(nz)
    spread = offsets[::-1]
    eig = basis.shape[1]
    width = weight.shape[1]
    per = groups // micro
    seq = per * low.shape[1]
    scatter_stage = jnp.where(k < EARLY_SCATTER, 0, 2)
    gather_stage = jnp.where(k < EARLY_GATHER, 0, 2)
    right, left = lax.rem(x + 1, nx), lax.rem(x + nx - 1, nx)
    across = lax.rem(x + 2, nx)
    first = k == sections - 1
    inner = k < sections - 1
    passes = k > 0

    def at_z(offset):
        return lax.rem(z + offset + nz, nz)

    def copy(src, dst, send, recv, device):
        return pltpu.make_async_remote_copy(
            src_ref=src, dst_ref=dst, send_sem=send, recv_sem=recv,
            device_id=device, device_id_type=MESH,
        )

    barrier = pltpu.get_barrier_semaphore()

    def greet(device):
        pl.semaphore_signal(barrier, inc=1, device_id=device, device_id_type=MESH)

    paired = {i: side for i, side in PAIRED.items() if i < nz}
    targets = sorted({(-offsets[i] % nz, side) for i, side in paired.items()})
    sources = sorted({(offsets[i] % nz, -side) for i, side in paired.items()})
    within = sorted({pair for pair in targets + sources if pair[0] != 0})

    def beside(side):
        return right if side > 0 else left

    for column in (right, left, across):
        greet((k, z, column))
    for offset in offsets[1:]:
        greet((k, at_z(offset), x))
    for offset, side in within:
        greet((k, at_z(offset), beside(side)))

    @pl.when(passes)
    def _():
        for offset in offsets:
            greet((k - 1, at_z(offset), x))
        for offset, side in targets:
            greet((k - 1, at_z(offset), beside(side)))

    @pl.when(inner)
    def _():
        for offset in offsets:
            greet((k + 1, at_z(offset), x))
        for offset, side in sources:
            greet((k + 1, at_z(offset), beside(side)))

    count = nx + nz - 2 + len(within)
    count = count + (nz + len(targets)) * passes.astype(jnp.int32)
    count = count + (nz + len(sources)) * inner.astype(jnp.int32)
    pl.semaphore_wait(barrier, count)
    loads[0].wait()

    def push(block, g, sent, section, start):
        for i in reversed(range(nz)):
            row = at_z(-offsets[i])
            if i >= start:
                copy(block, gath.at[g, x, z], sent, z_recv.at[g, i], (section, row, x)).start()
            if i in paired:
                copy(block, gath.at[g, x, z], sent, b_recv.at[g, i],
                     (section, row, beside(paired[i]))).start()

    def launch(g):
        push(top.at[g], g, t_send.at[g], k, 1)
        gath[g, x, z] = top[g]

    for early in range(LAUNCH):
        pl.when(first)(lambda early=early: launch(early))

    def multiply(g, column, table):
        total = None
        for zz in range(nz):
            start = pl.multiple_of((zz * nx + column) * width, width)
            part = jnp.dot(gath[g, column, zz], table[pl.ds(start, width), :],
                           preferred_element_type=jnp.float32)
            total = part if total is None else total + part
        return total

    def relay(g):
        for i, offset in enumerate(offsets):
            zz = at_z(offset)
            arrival = copy(low.at[g], gath.at[g, x, zz], z_send.at[g], z_recv.at[g, i], (k, z, x))
            if i == 0:
                pl.when(inner)(lambda: arrival.wait_recv())
            else:
                arrival.wait_recv()
            chunk = gath.at[g, x, zz]
            if i not in paired:
                copy(chunk, chunk, x_send.at[g], f_recv.at[g], (k, z, across)).start()
            if paired.get(i, -1) < 0:
                copy(chunk, chunk, x_send.at[g], p_recv.at[g], (k, z, right)).start()
            if paired.get(i, 1) > 0:
                copy(chunk, chunk, x_send.at[g], m_recv.at[g], (k, z, left)).start()
            if i in paired:
                side = paired[i]
                near = gath.at[g, beside(-side), zz]
                copy(near, near, x_send.at[g], b_recv.at[g, i], (k, z, right)).wait_recv()
                copy(near, near, x_send.at[g], f_recv.at[g], (k, z, beside(side))).start()

    def finish(g):
        @pl.when(passes)
        def _():
            acc[...] = multiply(g, x, weight)

        rights = sum(side > 0 for side in paired.values())
        for column, arrived, ready in ((left, p_recv, rights), (right, m_recv, len(paired) - rights)):
            whole = gath.at[g, column, pl.ds(0, nz - ready)]
            copy(whole, whole, x_send.at[g], arrived.at[g], (k, z, right)).wait_recv()

        @pl.when(passes)
        def _():
            acc[...] += multiply(g, left, weight) + multiply(g, right, weight)

        far = gath.at[g, across]
        copy(far, far, x_send.at[g], f_recv.at[g], (k, z, right)).wait_recv()

        @pl.when(passes)
        def _():
            through = acc[...] + multiply(g, across, weight)
            low[g] = (gath[g, x, z].astype(jnp.float32) + through).astype(low.dtype)
            push(low.at[g], g, z_send.at[g], k - 1, 0)

    def rotate(g, size):
        total = None
        for column in range(nx):
            for zz in range(nz):
                lhs = gath[pl.ds(g, size), column, zz]
                lhs = lhs.reshape(lhs.shape[0] * lhs.shape[1], width)
                part = jnp.dot(lhs, basis[(zz * nx + column) * width : (zz * nx + column + 1) * width, :],
                               preferred_element_type=jnp.float32)
                total = part if total is None else total + part
        rot[pl.ds(g, size)] = total.astype(rot.dtype).reshape(size, rot.shape[1], rot.shape[2])

    def rotated(m, column, half):
        rows = pl.ds(pl.multiple_of(m * seq, seq), seq)
        rhs = jnp.concatenate(
            [rot_in[column, 2 * half, rows], rot_in[column, 2 * half + 1, rows]], axis=1
        )
        return jnp.dot(rot_t[m], rhs, preferred_element_type=jnp.float32)

    def square_one(m):
        for step in range(nx * nz // 2):
            value = rotated(m, step // (nz // 2), step % (nz // 2))
            columns = slice(step * 2 * eig, (step + 1) * 2 * eig)
            before = jnp.where(m > 0, out[:, columns], 0.0)
            out[:, columns] = before + value * value

    def group_step(g, carry):
        pl.when(g + AHEAD < groups)(lambda: relay(g + AHEAD))
        pl.when(first & (g + LAUNCH < groups))(lambda: launch(g + LAUNCH))
        finish(g)

        @pl.when(lax.rem(g, per) == per - 1)
        def _():
            m = g // per
            rotate(m * per, per)
            tokens = rot[pl.ds(m * per, per)].reshape(seq, eig)
            rot_t[m] = (tokens.astype(jnp.float32) * (1.0 / 16.0)).T.astype(rot_t.dtype)
            pl.when(gather_stage == 0)(lambda: square_one(m))
        return carry

    def chain():
        for early in range(AHEAD):
            relay(early)
        loads[3].wait()
        loads[4].wait()
        lax.fori_loop(0, groups, group_step, 0)

    def product(owner, zz):
        start = pl.multiple_of((owner * nz + zz) * eig, eig)
        piece = jnp.dot(act[...], basis_in[:, pl.ds(start, eig)], preferred_element_type=jnp.float32)
        part[owner, zz] = piece.astype(part.dtype)

    def reduce_scatter():
        loads[1].wait()
        loads[2].wait()
        for i, offset in enumerate(spread):
            zz = at_z(offset)
            product(across, zz)
            copy(part.at[across, zz], far_in.at[i], rf_send, rf_recv.at[i],
                 (k, z, left if i % 2 == 0 else right)).start()
        for i, offset in enumerate(spread):
            zz = at_z(offset)
            product(left, zz)
            product(right, zz)
            if i % 2 == 0:
                copy(part.at[right, zz], near_in.at[0, i], rn_send, rn_recv.at[0, i], (k, z, right)).start()
            else:
                copy(part.at[left, zz], near_in.at[1, i], rn_send, rn_recv.at[1, i], (k, z, left)).start()
        for i, offset in enumerate(spread):
            zz = at_z(offset)
            product(x, zz)
            copy(far_in.at[i], far_in.at[i], rf_send, rf_recv.at[i], (k, z, left)).wait_recv()
            if i % 2 == 0:
                part[left, zz] = add(part[left, zz], far_in[i])
                copy(part.at[left, zz], near_in.at[1, i], rn_send, rn_recv.at[1, i], (k, z, left)).start()
            else:
                part[right, zz] = add(part[right, zz], far_in[i])
                copy(part.at[right, zz], near_in.at[0, i], rn_send, rn_recv.at[0, i], (k, z, right)).start()
        for i, offset in enumerate(spread):
            zz = at_z(offset)
            for side in range(2):
                arrived = near_in.at[side, i]
                copy(arrived, arrived, rn_send, rn_recv.at[side, i], (k, z, left)).wait_recv()
            part[x, zz] = add(part[x, zz], near_in[0, i], near_in[1, i])
            if offset != 0:
                copy(part.at[x, zz], z_in.at[i], rz_send, rz_recv.at[i], (k, zz, x)).start()
        total = part[x, z].astype(jnp.float32)
        for i, offset in enumerate(spread):
            if offset != 0:
                copy(z_in.at[i], z_in.at[i], rz_send, rz_recv.at[i], (k, z, left)).wait_recv()
                total = total + z_in[i].astype(jnp.float32)
        rot_in[x, z] = total.astype(rot_in.dtype)

    def add(*terms):
        total = terms[0].astype(jnp.float32)
        for term in terms[1:]:
            total = total + term.astype(jnp.float32)
        return total.astype(part.dtype)

    def run(body):
        lax.fori_loop(0, nz // 2, body, 0)

    def square_column(column):
        def square(half, carry):
            total = None
            for m in range(micro):
                value = rotated(m, column, half)
                total = value * value if total is None else total + value * value
            start = pl.multiple_of((column * nz + 2 * half) * eig, 2 * eig)
            out[:, pl.ds(start, 2 * eig)] = total
            return carry

        pl.when(gather_stage > 0)(lambda: run(square))

    def all_gather():
        mine = rot_in.at[x, z]
        for i in reversed(range(1, nz)):
            copy(mine, mine, az_send, az_recv.at[i], (k, at_z(-offsets[i]), x)).start()
        for i, offset in enumerate(offsets):
            piece = rot_in.at[x, at_z(offset)]
            if i > 0:
                copy(piece, piece, az_send, az_recv.at[i], (k, z, right)).wait_recv()
            copy(piece, piece, ax_send, ap_recv.at[i], (k, z, right)).start()
            copy(piece, piece, ax_send, am_recv.at[i], (k, z, left)).start()
        for i, offset in enumerate(offsets):
            zz = at_z(offset)
            from_left, from_right = rot_in.at[left, zz], rot_in.at[right, zz]
            copy(from_left, from_left, ax_send, ap_recv.at[i], (k, z, right)).wait_recv()
            if i % 2 == 0:
                copy(from_left, from_left, ax_send, af_recv, (k, z, right)).start()
            copy(from_right, from_right, ax_send, am_recv.at[i], (k, z, left)).wait_recv()
            if i % 2 == 1:
                copy(from_right, from_right, ax_send, af_recv, (k, z, left)).start()
        for column in (x, left, right):
            square_column(column)
        whole = rot_in.at[across]
        copy(whole, whole, ax_send, af_recv, (k, z, left)).wait_recv()
        square_column(across)

    def stage(index, carry):
        pl.when(index == scatter_stage)(reduce_scatter)
        pl.when(index == gather_stage)(all_gather)
        pl.when(index == 1)(chain)
        return carry

    lax.fori_loop(0, 3, stage, 0)

    for pieces, sem in (
        (part.at[0], rf_send), (part.at[pl.ds(0, 2)], rn_send), (part.at[0, pl.ds(0, nz - 1)], rz_send),
        (part.at[0, pl.ds(0, nz - 1)], az_send), (part.at[pl.ds(0, 3)], ax_send),
    ):
        copy(pieces, pieces, sem, af_recv, (k, z, right)).wait_send()

    def drain(g, carry):
        def sent(sem, *sizes):
            for columns, rows in sizes:
                if columns and rows:
                    block = gath.at[g, pl.ds(0, columns), pl.ds(0, rows)]
                    copy(block, block, sem.at[g], f_recv.at[g], (k, z, right)).wait_send()

        sent(x_send, (3, nz - len(paired)), (2, len(paired)))
        pl.when(passes)(lambda: sent(z_send, (1, nz), (1, len(paired))))
        pl.when(first)(lambda: sent(t_send, (1, nz - 1), (1, len(paired))))
        return carry

    lax.fori_loop(0, groups, drain, 0)


def run_fused(sections, nz, nx, act, top, weight, basis, basis_in):
    micro, seq, feat = top.shape
    groups = GROUPS
    tokens = micro * seq
    rows = tokens // groups
    eig = basis.shape[1]
    half = jnp.bfloat16
    dma = pltpu.SemaphoreType.DMA
    return pl.pallas_call(
        functools.partial(fused_kernel, sections, nz, nx, groups, micro),
        out_shape=jax.ShapeDtypeStruct((eig, nx * nz * eig), jnp.float32),
        in_specs=[pl.BlockSpec(memory_space=pltpu.HBM)] * 5,
        out_specs=pl.BlockSpec(memory_space=pltpu.VMEM),
        scratch_shapes=[
            pltpu.VMEM((tokens, feat), half),
            pltpu.VMEM((groups, rows, feat), half),
            pltpu.VMEM(weight.shape, half),
            pltpu.VMEM(basis.shape, half),
            pltpu.VMEM(basis_in.shape, half),
            pltpu.VMEM((groups, nx, nz, rows, feat), half),
            pltpu.VMEM((groups, rows, feat), half),
            pltpu.VMEM((rows, feat), jnp.float32),
            pltpu.VMEM((groups, rows, eig), half),
            pltpu.VMEM((micro, eig, seq), half),
            pltpu.VMEM((nx, nz, tokens, eig), half),
            pltpu.VMEM((nz, tokens, eig), half),
            pltpu.VMEM((2, nz, tokens, eig), half),
            pltpu.VMEM((nz, tokens, eig), half),
            pltpu.VMEM((nx, nz, tokens, eig), half),
            dma((5,)),
            dma((groups, nz)), dma((groups, nz)), dma((groups,)), dma((groups,)), dma((groups,)),
            dma((groups,)), dma((groups,)), dma((groups,)),
            dma((nz,)), dma((2, nz)), dma((nz,)), dma, dma, dma,
            dma((nz,)), dma((nz,)), dma((nz,)), dma, dma, dma,
        ],
        compiler_params=pltpu.CompilerParams(
            collective_id=0, has_side_effects=True, vmem_limit_bytes=VMEM_LIMIT
        ),
        name="fused",
    )(*(pltpu.with_memory_space_constraint(a, pltpu.HBM) for a in (
        act.reshape(tokens, feat), top.reshape(groups, rows, feat), weight, basis, basis_in)))


def per_device(sections, nz, nx, activations, top_grad, projection, basis_out, basis_in):
    return run_fused(
        sections, nz, nx, activations[0], top_grad, projection[0], basis_out[0], basis_in[0]
    )[None]


def solution(mesh):
    sections = mesh.shape["section"]
    nx = 4
    nz = mesh.shape["shard"] // nx
    finer = Mesh(mesh.devices.reshape(sections, nz, nx), ("section", "shard_0", "shard_1"))
    in_specs = (
        P("section", None, None, SHARD),
        P(None, None, SHARD),
        P("section", None, SHARD),
        P("section", None, SHARD),
        P("section", SHARD, None),
    )
    out_specs = P("section", SHARD, None)
    return jax.shard_map(
        functools.partial(per_device, sections, nz, nx), mesh=finer, in_specs=in_specs,
        out_specs=out_specs, check_vma=False,
    )
```

```python
import functools

import jax
import jax.numpy as jnp
from jax import lax
from jax.experimental import pallas as pl
from jax.experimental.pallas import tpu as pltpu
from jax.sharding import Mesh
from jax.sharding import PartitionSpec as P

MESH = pl.DeviceIdType.MESH
SHARD = ("shard_0", "shard_1")
GROUPS = 16
EARLY_SCATTER = 4
EARLY_GATHER = 2
AHEAD = 2
LAUNCH = 4
VMEM_LIMIT = 26 << 20
PAIRED = {0: 1, 1: 1, 2: -1}


def ring_order(size):
    near = [d for i in range(1, (size + 1) // 2) for d in (i, -i)]
    return [0] + near + ([size // 2] if size % 2 == 0 else [])


def fused_kernel(sections, nz, nx, groups, micro, act_hbm, top_hbm, weight_hbm, basis_hbm, in_hbm, out,
                 act, top, weight, basis, basis_in, gath, low, acc, rot, rot_t,
                 part, far_in, near_in, z_in, rot_in, load,
                 z_recv, b_recv, p_recv, m_recv, f_recv, t_send, z_send, x_send,
                 rf_recv, rn_recv, rz_recv, rf_send, rn_send, rz_send,
                 az_recv, ap_recv, am_recv, af_recv, az_send, ax_send):
    k = lax.axis_index("section")
    z = lax.axis_index("shard_0")
    x = lax.axis_index("shard_1")
    loads = [
        pltpu.make_async_copy(src, dst, load.at[i])
        for i, (src, dst) in enumerate(
            ((top_hbm, top), (act_hbm, act), (in_hbm, basis_in), (weight_hbm, weight), (basis_hbm, basis))
        )
    ]
    for copy_in in loads:
        copy_in.start()
    offsets = ring_order(nz)
    spread = offsets[::-1]
    eig = basis.shape[1]
    width = weight.shape[1]
    per = groups // micro
    seq = per * low.shape[1]
    scatter_stage = jnp.where(k < EARLY_SCATTER, 0, 2)
    gather_stage = jnp.where(k < EARLY_GATHER, 0, 2)
    right, left = lax.rem(x + 1, nx), lax.rem(x + nx - 1, nx)
    across = lax.rem(x + 2, nx)
    first = k == sections - 1
    inner = k < sections - 1
    passes = k > 0

    def at_z(offset):
        return lax.rem(z + offset + nz, nz)

    def copy(src, dst, send, recv, device):
        return pltpu.make_async_remote_copy(
            src_ref=src, dst_ref=dst, send_sem=send, recv_sem=recv,
            device_id=device, device_id_type=MESH,
        )

    barrier = pltpu.get_barrier_semaphore()

    def greet(device):
        pl.semaphore_signal(barrier, inc=1, device_id=device, device_id_type=MESH)

    paired = {i: side for i, side in PAIRED.items() if i < nz}
    targets = sorted({(-offsets[i] % nz, side) for i, side in paired.items()})
    sources = sorted({(offsets[i] % nz, -side) for i, side in paired.items()})
    within = sorted({pair for pair in targets + sources if pair[0] != 0})

    def beside(side):
        return right if side > 0 else left

    for column in (right, left, across):
        greet((k, z, column))
    for offset in offsets[1:]:
        greet((k, at_z(offset), x))
    for offset, side in within:
        greet((k, at_z(offset), beside(side)))

    @pl.when(passes)
    def _():
        for offset in offsets:
            greet((k - 1, at_z(offset), x))
        for offset, side in targets:
            greet((k - 1, at_z(offset), beside(side)))

    @pl.when(inner)
    def _():
        for offset in offsets:
            greet((k + 1, at_z(offset), x))
        for offset, side in sources:
            greet((k + 1, at_z(offset), beside(side)))

    count = nx + nz - 2 + len(within)
    count = count + (nz + len(targets)) * passes.astype(jnp.int32)
    count = count + (nz + len(sources)) * inner.astype(jnp.int32)
    pl.semaphore_wait(barrier, count)
    loads[0].wait()

    def push(block, g, sent, section, start):
        for i in reversed(range(nz)):
            row = at_z(-offsets[i])
            if i >= start:
                copy(block, gath.at[g, x, z], sent, z_recv.at[g, i], (section, row, x)).start()
            if i in paired:
                copy(block, gath.at[g, x, z], sent, b_recv.at[g, i],
                     (section, row, beside(paired[i]))).start()

    def launch(g):
        push(top.at[g], g, t_send.at[g], k, 1)
        gath[g, x, z] = top[g]

    for early in range(LAUNCH):
        pl.when(first)(lambda early=early: launch(early))

    def multiply(g, column, table):
        total = None
        for zz in range(nz):
            start = pl.multiple_of((zz * nx + column) * width, width)
            part = jnp.dot(gath[g, column, zz], table[pl.ds(start, width), :],
                           preferred_element_type=jnp.float32)
            total = part if total is None else total + part
        return total

    def relay(g):
        for i, offset in enumerate(offsets):
            zz = at_z(offset)
            arrival = copy(low.at[g], gath.at[g, x, zz], z_send.at[g], z_recv.at[g, i], (k, z, x))
            if i == 0:
                pl.when(inner)(lambda: arrival.wait_recv())
            else:
                arrival.wait_recv()
            chunk = gath.at[g, x, zz]
            if i not in paired:
                copy(chunk, chunk, x_send.at[g], f_recv.at[g], (k, z, across)).start()
            if paired.get(i, -1) < 0:
                copy(chunk, chunk, x_send.at[g], p_recv.at[g], (k, z, right)).start()
            if paired.get(i, 1) > 0:
                copy(chunk, chunk, x_send.at[g], m_recv.at[g], (k, z, left)).start()
            if i in paired:
                side = paired[i]
                near = gath.at[g, beside(-side), zz]
                copy(near, near, x_send.at[g], b_recv.at[g, i], (k, z, right)).wait_recv()
                copy(near, near, x_send.at[g], f_recv.at[g], (k, z, beside(side))).start()

    def finish(g):
        @pl.when(passes)
        def _():
            acc[...] = multiply(g, x, weight)

        rights = sum(side > 0 for side in paired.values())
        for column, arrived, ready in ((left, p_recv, rights), (right, m_recv, len(paired) - rights)):
            whole = gath.at[g, column, pl.ds(0, nz - ready)]
            copy(whole, whole, x_send.at[g], arrived.at[g], (k, z, right)).wait_recv()

        @pl.when(passes)
        def _():
            acc[...] += multiply(g, left, weight) + multiply(g, right, weight)

        far = gath.at[g, across]
        copy(far, far, x_send.at[g], f_recv.at[g], (k, z, right)).wait_recv()

        @pl.when(passes)
        def _():
            through = acc[...] + multiply(g, across, weight)
            low[g] = (gath[g, x, z].astype(jnp.float32) + through).astype(low.dtype)
            push(low.at[g], g, z_send.at[g], k - 1, 0)

    def rotate(g, size):
        total = None
        for column in range(nx):
            for zz in range(nz):
                lhs = gath[pl.ds(g, size), column, zz]
                lhs = lhs.reshape(lhs.shape[0] * lhs.shape[1], width)
                part = jnp.dot(lhs, basis[(zz * nx + column) * width : (zz * nx + column + 1) * width, :],
                               preferred_element_type=jnp.float32)
                total = part if total is None else total + part
        rot[pl.ds(g, size)] = total.astype(rot.dtype).reshape(size, rot.shape[1], rot.shape[2])

    def rotated(m, column, half):
        rows = pl.ds(pl.multiple_of(m * seq, seq), seq)
        rhs = jnp.concatenate(
            [rot_in[column, 2 * half, rows], rot_in[column, 2 * half + 1, rows]], axis=1
        )
        return jnp.dot(rot_t[m], rhs, preferred_element_type=jnp.float32)

    def square_one(m):
        for step in range(nx * nz // 2):
            value = rotated(m, step // (nz // 2), step % (nz // 2))
            columns = slice(step * 2 * eig, (step + 1) * 2 * eig)
            before = jnp.where(m > 0, out[:, columns], 0.0)
            out[:, columns] = before + value * value

    def group_step(g, carry):
        pl.when(g + AHEAD < groups)(lambda: relay(g + AHEAD))
        pl.when(first & (g + LAUNCH < groups))(lambda: launch(g + LAUNCH))
        finish(g)

        @pl.when(lax.rem(g, per) == per - 1)
        def _():
            m = g // per
            rotate(m * per, per)
            tokens = rot[pl.ds(m * per, per)].reshape(seq, eig)
            rot_t[m] = (tokens.astype(jnp.float32) * (1.0 / 16.0)).T.astype(rot_t.dtype)
            pl.when(gather_stage == 0)(lambda: square_one(m))
        return carry

    def chain():
        for early in range(AHEAD):
            relay(early)
        loads[3].wait()
        loads[4].wait()
        lax.fori_loop(0, groups, group_step, 0)

    def product(owner, zz):
        start = pl.multiple_of((owner * nz + zz) * eig, eig)
        piece = jnp.dot(act[...], basis_in[:, pl.ds(start, eig)], preferred_element_type=jnp.float32)
        part[owner, zz] = piece.astype(part.dtype)

    def reduce_scatter():
        loads[1].wait()
        loads[2].wait()
        for i, offset in enumerate(spread):
            zz = at_z(offset)
            product(across, zz)
            copy(part.at[across, zz], far_in.at[i], rf_send, rf_recv.at[i],
                 (k, z, left if i % 2 == 0 else right)).start()
        for i, offset in enumerate(spread):
            zz = at_z(offset)
            product(left, zz)
            product(right, zz)
            if i % 2 == 0:
                copy(part.at[right, zz], near_in.at[0, i], rn_send, rn_recv.at[0, i], (k, z, right)).start()
            else:
                copy(part.at[left, zz], near_in.at[1, i], rn_send, rn_recv.at[1, i], (k, z, left)).start()
        for i, offset in enumerate(spread):
            zz = at_z(offset)
            product(x, zz)
            copy(far_in.at[i], far_in.at[i], rf_send, rf_recv.at[i], (k, z, left)).wait_recv()
            if i % 2 == 0:
                part[left, zz] = add(part[left, zz], far_in[i])
                copy(part.at[left, zz], near_in.at[1, i], rn_send, rn_recv.at[1, i], (k, z, left)).start()
            else:
                part[right, zz] = add(part[right, zz], far_in[i])
                copy(part.at[right, zz], near_in.at[0, i], rn_send, rn_recv.at[0, i], (k, z, right)).start()
        for i, offset in enumerate(spread):
            zz = at_z(offset)
            for side in range(2):
                arrived = near_in.at[side, i]
                copy(arrived, arrived, rn_send, rn_recv.at[side, i], (k, z, left)).wait_recv()
            part[x, zz] = add(part[x, zz], near_in[0, i], near_in[1, i])
            if offset != 0:
                copy(part.at[x, zz], z_in.at[i], rz_send, rz_recv.at[i], (k, zz, x)).start()
        total = part[x, z].astype(jnp.float32)
        for i, offset in enumerate(spread):
            if offset != 0:
                copy(z_in.at[i], z_in.at[i], rz_send, rz_recv.at[i], (k, z, left)).wait_recv()
                total = total + z_in[i].astype(jnp.float32)
        rot_in[x, z] = total.astype(rot_in.dtype)

    def add(*terms):
        total = terms[0].astype(jnp.float32)
        for term in terms[1:]:
            total = total + term.astype(jnp.float32)
        return total.astype(part.dtype)

    def run(body):
        lax.fori_loop(0, nz // 2, body, 0)

    def square_column(column):
        def square(half, carry):
            total = None
            for m in range(micro):
                value = rotated(m, column, half)
                total = value * value if total is None else total + value * value
            start = pl.multiple_of((column * nz + 2 * half) * eig, 2 * eig)
            out[:, pl.ds(start, 2 * eig)] = total
            return carry

        pl.when(gather_stage > 0)(lambda: run(square))

    def all_gather():
        mine = rot_in.at[x, z]
        for i in reversed(range(1, nz)):
            copy(mine, mine, az_send, az_recv.at[i], (k, at_z(-offsets[i]), x)).start()
        for i, offset in enumerate(offsets):
            piece = rot_in.at[x, at_z(offset)]
            if i > 0:
                copy(piece, piece, az_send, az_recv.at[i], (k, z, right)).wait_recv()
            copy(piece, piece, ax_send, ap_recv.at[i], (k, z, right)).start()
            copy(piece, piece, ax_send, am_recv.at[i], (k, z, left)).start()
        for i, offset in enumerate(offsets):
            zz = at_z(offset)
            from_left, from_right = rot_in.at[left, zz], rot_in.at[right, zz]
            copy(from_left, from_left, ax_send, ap_recv.at[i], (k, z, right)).wait_recv()
            if i % 2 == 0:
                copy(from_left, from_left, ax_send, af_recv, (k, z, right)).start()
            copy(from_right, from_right, ax_send, am_recv.at[i], (k, z, left)).wait_recv()
            if i % 2 == 1:
                copy(from_right, from_right, ax_send, af_recv, (k, z, left)).start()
        for column in (x, left, right):
            square_column(column)
        whole = rot_in.at[across]
        copy(whole, whole, ax_send, af_recv, (k, z, left)).wait_recv()
        square_column(across)

    def stage(index, carry):
        pl.when(index == scatter_stage)(reduce_scatter)
        pl.when(index == gather_stage)(all_gather)
        pl.when(index == 1)(chain)
        return carry

    lax.fori_loop(0, 3, stage, 0)

    for pieces, sem in (
        (part.at[0], rf_send), (part.at[pl.ds(0, 2)], rn_send), (part.at[0, pl.ds(0, nz - 1)], rz_send),
        (part.at[0, pl.ds(0, nz - 1)], az_send), (part.at[pl.ds(0, 3)], ax_send),
    ):
        copy(pieces, pieces, sem, af_recv, (k, z, right)).wait_send()

    def drain(g, carry):
        def sent(sem, *sizes):
            for columns, rows in sizes:
                if columns and rows:
                    block = gath.at[g, pl.ds(0, columns), pl.ds(0, rows)]
                    copy(block, block, sem.at[g], f_recv.at[g], (k, z, right)).wait_send()

        sent(x_send, (3, nz - len(paired)), (2, len(paired)))
        pl.when(passes)(lambda: sent(z_send, (1, nz), (1, len(paired))))
        pl.when(first)(lambda: sent(t_send, (1, nz - 1), (1, len(paired))))
        return carry

    lax.fori_loop(0, groups, drain, 0)


def run_fused(sections, nz, nx, act, top, weight, basis, basis_in):
    micro, seq, feat = top.shape
    groups = GROUPS
    tokens = micro * seq
    rows = tokens // groups
    eig = basis.shape[1]
    half = jnp.bfloat16
    dma = pltpu.SemaphoreType.DMA
    return pl.pallas_call(
        functools.partial(fused_kernel, sections, nz, nx, groups, micro),
        out_shape=jax.ShapeDtypeStruct((eig, nx * nz * eig), jnp.float32),
        in_specs=[pl.BlockSpec(memory_space=pltpu.HBM)] * 5,
        out_specs=pl.BlockSpec(memory_space=pltpu.VMEM),
        scratch_shapes=[
            pltpu.VMEM((tokens, feat), half),
            pltpu.VMEM((groups, rows, feat), half),
            pltpu.VMEM(weight.shape, half),
            pltpu.VMEM(basis.shape, half),
            pltpu.VMEM(basis_in.shape, half),
            pltpu.VMEM((groups, nx, nz, rows, feat), half),
            pltpu.VMEM((groups, rows, feat), half),
            pltpu.VMEM((rows, feat), jnp.float32),
            pltpu.VMEM((groups, rows, eig), half),
            pltpu.VMEM((micro, eig, seq), half),
            pltpu.VMEM((nx, nz, tokens, eig), half),
            pltpu.VMEM((nz, tokens, eig), half),
            pltpu.VMEM((2, nz, tokens, eig), half),
            pltpu.VMEM((nz, tokens, eig), half),
            pltpu.VMEM((nx, nz, tokens, eig), half),
            dma((5,)),
            dma((groups, nz)), dma((groups, nz)), dma((groups,)), dma((groups,)), dma((groups,)),
            dma((groups,)), dma((groups,)), dma((groups,)),
            dma((nz,)), dma((2, nz)), dma((nz,)), dma, dma, dma,
            dma((nz,)), dma((nz,)), dma((nz,)), dma, dma, dma,
        ],
        compiler_params=pltpu.CompilerParams(
            collective_id=0, has_side_effects=True, vmem_limit_bytes=VMEM_LIMIT
        ),
        name="fused",
    )(*(pltpu.with_memory_space_constraint(a, pltpu.HBM) for a in (
        act.reshape(tokens, feat), top.reshape(groups, rows, feat), weight, basis, basis_in)))


def per_device(sections, nz, nx, activations, top_grad, projection, basis_out, basis_in):
    return run_fused(
        sections, nz, nx, activations[0], top_grad, projection[0], basis_out[0], basis_in[0]
    )[None]


def solution(mesh):
    sections = mesh.shape["section"]
    nx = 4
    nz = mesh.shape["shard"] // nx
    finer = Mesh(mesh.devices.reshape(sections, nz, nx), ("section", "shard_0", "shard_1"))
    in_specs = (
        P("section", None, None, SHARD),
        P(None, None, SHARD),
        P("section", None, SHARD),
        P("section", None, SHARD),
        P("section", SHARD, None),
    )
    out_specs = P("section", SHARD, None)
    return jax.shard_map(
        functools.partial(per_device, sections, nz, nx), mesh=finer, in_specs=in_specs,
        out_specs=out_specs, check_vma=False,
    )
```
